128 devices in a mesh: seq: 32 (over x, z, core), head: 4 (over y).
Axes of the slice: x: 4, y: 4, z: 4, core: 2. Of those that a mesh axis runs over, the one named last changes fastest.
Arguments:
- q_in: bfloat16 [65536, 2048], P(('seq', 'head')), may hold values from -6 to 6
- k_in: bfloat16 [65536, 2048], P(('seq', 'head')), may hold values from -6 to 6
- v_in: bfloat16 [65536, 2048], P(('seq', 'head')), may hold values from -6 to 6
- beta: bfloat16 [65536, 16], P(('seq', 'head')), may hold values from 0 to 1, as said below
- conv_q: float32 [4, 2048], replicated, may hold values from -3 to 3
- conv_k: float32 [4, 2048], replicated, may hold values from -3 to 3
- conv_v: float32 [4, 2048], replicated, may hold values from -3 to 3
- out_gain: float32 [128], replicated, may hold values from 0.25 to 1.75
Outputs:
- mixed: bfloat16 [65536, 2048], P(('seq', 'head'))
The draws below stay inside these ranges and needn't reach their ends.
Inputs may be any that keep to these rules, and one draw needn't show every extreme that they name: `beta`: write strengths of the delta rule, positive.
All inputs are finite; a program needn't handle non-finite values.
Results may differ from the reference program's by a relative error of at most 0.001.
Values may be sent and summed in bfloat16 or wider, within the bound.
No kernel may reach another device: no remote copies, remote signals or barrier semaphores. Data moves between devices by JAX's collectives and lax.ppermute only.
A program may use at most 576 MiB of HBM per device.

```python
import math
import jax
import jax.numpy as jnp
from jax import lax

HEAD_NUMBER = 16
KEY_WIDTH = 128
DV = 128
BLOCK = 64
KW = 4
TRACE_TOKENS = 65536


def draw_beta(key, part):
    key_order = jax.random.fold_in(key, 11)
    key_slow = jax.random.fold_in(key, 12)
    key_fast = jax.random.fold_in(key, 13)
    key_jitter = jax.random.fold_in(key, 14)
    surge_seed = jax.random.fold_in(key, 15)
    level_seed = jax.random.fold_in(key, 16)
    plateau_seed = jax.random.fold_in(key, 17)
    plateau_level_seed = jax.random.fold_in(key, 18)
    rank_order = jax.random.permutation(key_order, HEAD_NUMBER)
    sluggish_heads = rank_order < HEAD_NUMBER // 2
    slow_rate = jax.random.uniform(key_slow, (HEAD_NUMBER,), jnp.float32, 0.2, 1.0) * (KEY_WIDTH / TRACE_TOKENS)
    fast_rate = jnp.exp(jax.random.uniform(key_fast, (HEAD_NUMBER,), jnp.float32, math.log(0.1), math.log(0.9)))
    head_rate = jnp.where(sluggish_heads, slow_rate, fast_rate)
    jitter = jax.random.uniform(key_jitter, (TRACE_TOKENS, HEAD_NUMBER), jnp.float32, 0.5, 1.5)
    surge_strength = head_rate[None, :] * jitter
    token_places = jnp.arange(TRACE_TOKENS)
    plateau_span = 4 * BLOCK
    slot_count = TRACE_TOKENS // plateau_span
    plateau_count = max(TRACE_TOKENS // (64 * BLOCK), 1)
    chosen_slots = jax.random.permutation(plateau_seed, slot_count)[:plateau_count]
    token_slot = token_places // plateau_span
    within_plateau = jnp.any(token_slot[:, None] == chosen_slots[None, :], axis=1)
    plateau_height = jax.random.uniform(plateau_level_seed, (TRACE_TOKENS, HEAD_NUMBER), jnp.float32, 0.016, 0.0196)
    surge_strength = jnp.where(within_plateau[:, None] & sluggish_heads[None, :], plateau_height, surge_strength)
    surge_length = max(KEY_WIDTH // 4, 2)
    surge_onset = jax.random.randint(surge_seed, (4,), 0, TRACE_TOKENS - surge_length)
    within_surge = jnp.any((token_places[:, None] >= surge_onset[None, :]) & (token_places[:, None] < surge_onset[None, :] + surge_length), axis=1)
    surge_height = jax.random.uniform(level_seed, (TRACE_TOKENS, HEAD_NUMBER), jnp.float32, 0.5, 1.0)
    surge_strength = jnp.where(within_surge[:, None] & sluggish_heads[None, :], surge_height, surge_strength)
    return jnp.minimum(surge_strength, 1.0).astype(jnp.bfloat16)


def block_scale(key, shape, cuts, least, largest):
    level = 1.0
    for position, blocks in cuts:
        draws = jax.random.uniform(jax.random.fold_in(jax.random.fold_in(key, 6), position), (blocks,), jnp.float32, least / len(cuts), largest / len(cuts))
        level = level * jnp.repeat(jnp.exp(draws), shape[position] // blocks).reshape((-1,) + (1,) * (len(shape) - 1 - position))
    return level


def bell_draw(rng, shape, spread, bound, shards=(), held_as=jnp.bfloat16):
    level = block_scale(rng, shape, shards, -0.22, 0.18) if shards else 1.0
    result = jax.random.normal(rng, shape, jnp.float32) * spread * level
    return jnp.minimum(jnp.maximum(result, -bound), bound).astype(held_as)


def setup_inputs(seed: int = 0) -> dict:
    keys = jax.random.split(jax.random.key(seed), 9)
    return {
        "q_in": bell_draw(keys[0], (TRACE_TOKENS, HEAD_NUMBER * KEY_WIDTH), 1.0, 6.0, ((0, 128),)),
        "k_in": bell_draw(keys[1], (TRACE_TOKENS, HEAD_NUMBER * KEY_WIDTH), 1.0, 6.0, ((0, 128),)),
        "v_in": bell_draw(keys[2], (TRACE_TOKENS, HEAD_NUMBER * DV), 1.0, 6.0, ((0, 128),)),
        "beta": draw_beta(jax.random.fold_in(keys[8], 71), 0),
        "conv_q": bell_draw(keys[4], (KW, HEAD_NUMBER * KEY_WIDTH), KW ** -0.5, 3.0, (), jnp.float32),
        "conv_k": bell_draw(keys[5], (KW, HEAD_NUMBER * KEY_WIDTH), KW ** -0.5, 3.0, (), jnp.float32),
        "conv_v": bell_draw(keys[6], (KW, HEAD_NUMBER * DV), KW ** -0.5, 3.0, (), jnp.float32),
        "out_gain": jnp.clip(1.0 + 0.15 * jax.random.normal(keys[7], (DV,), jnp.float32), 0.25, 1.75),
    }


peak_level = lax.Precision.HIGHEST

def causal_conv(padded, weight, length):
    summed = weight[0] * padded[0:length]
    for offset in range(1, weight.shape[0]):
        summed = summed + weight[offset] * padded[offset:offset + length]
    return summed

def unit_rows(vectors):
    return vectors / jnp.sqrt(lax.optimization_barrier(jnp.sum(vectors * vectors, axis=-1, keepdims=True)) + 1e-06)

def features(q_pad, k_pad, v_pad, beta_rows, conv_q, conv_k, conv_v):
    length = beta_rows.shape[0]
    head_count = beta_rows.shape[1]
    q_conv = causal_conv(q_pad.astype(jnp.float32), conv_q, length)
    k_conv = causal_conv(k_pad.astype(jnp.float32), conv_k, length)
    v_conv = causal_conv(v_pad.astype(jnp.float32), conv_v, length)
    queries = unit_rows(jax.nn.silu(q_conv).reshape(length, head_count, -1))
    key_rows = unit_rows(jax.nn.silu(k_conv).reshape(length, head_count, -1))
    values = jax.nn.silu(v_conv).reshape(length, head_count, -1)
    return (queries, key_rows, values, beta_rows.astype(jnp.float32))

def block_parts(queries, key_rows, values, surge_strength):
    length, head_count, ignored = key_rows.shape
    block_count = length // BLOCK

    def to_blocks(matrix):
        return jnp.swapaxes(matrix.reshape(block_count, BLOCK, head_count, matrix.shape[-1]), 1, 2)
    query_tiles = to_blocks(queries)
    key_tiles = to_blocks(key_rows)
    v_blocks = to_blocks(values)
    s_blocks = jnp.swapaxes(surge_strength.reshape(block_count, BLOCK, head_count), 1, 2)[..., None]
    scaled_k = key_tiles * s_blocks
    gram_rows = jnp.einsum('nhik,nhjk->nhij', scaled_k, key_tiles, precision=peak_level)
    system = jnp.tril(gram_rows, -1) + jnp.eye(BLOCK, dtype=gram_rows.dtype)
    weight_rows = lax.linalg.triangular_solve(system, scaled_k, left_side=True, lower=True, unit_diagonal=True)
    update_rows = lax.linalg.triangular_solve(system, v_blocks * s_blocks, left_side=True, lower=True, unit_diagonal=True)
    attention_scores = jnp.tril(jnp.einsum('nhik,nhjk->nhij', query_tiles, key_tiles, precision=peak_level))
    return (query_tiles, key_tiles, weight_rows, update_rows, attention_scores)

def run_blocks(carried, parts):

    def advance(present_value, pieces):
        query_tiles, key_tiles, weight_rows, update_rows, attention_scores = pieces
        fresh_values = update_rows - jnp.einsum('jel,jlm->jem', weight_rows, present_value, precision=peak_level)
        blended_rows = jnp.einsum('jel,jlm->jem', query_tiles, present_value, precision=peak_level) + jnp.einsum('ezq,eqd->ezd', attention_scores, fresh_values, precision=peak_level)
        present_value = present_value + jnp.einsum('pty,ptn->pyn', key_tiles, fresh_values, precision=peak_level)
        return (present_value, blended_rows)
    ignored, outputs = lax.scan(advance, carried, parts)
    block_count, head_count, rows_block, width = outputs.shape
    return jnp.swapaxes(outputs, 1, 2).reshape(block_count * rows_block, head_count, width)

def finish(outputs, out_gain):
    inv_rms = lax.rsqrt(lax.optimization_barrier(jnp.mean(outputs * outputs, axis=-1, keepdims=True)) + 1e-05)
    return (outputs * inv_rms * out_gain).reshape(outputs.shape[0], -1).astype(jnp.bfloat16)

def reference(q_in, k_in, v_in, beta, conv_q, conv_k, conv_v, out_gain):
    pad_rows = jnp.zeros((KW - 1, q_in.shape[1]), q_in.dtype)
    pad_vals = jnp.zeros((KW - 1, v_in.shape[1]), v_in.dtype)
    q_pad = jnp.concatenate([pad_rows, q_in], axis=0)
    k_pad = jnp.concatenate([pad_rows, k_in], axis=0)
    v_pad = jnp.concatenate([pad_vals, v_in], axis=0)
    queries, key_rows, values, surge_strength = features(q_pad, k_pad, v_pad, beta, conv_q, conv_k, conv_v)
    parts = block_parts(queries, key_rows, values, surge_strength)
    carried = jnp.zeros((HEAD_NUMBER, KEY_WIDTH, DV), jnp.float32)
    return finish(run_blocks(carried, parts), out_gain)
```

```python
import functools

import jax
import jax.numpy as jnp
from jax import lax
from jax.experimental import pallas as pl
from jax.experimental.pallas import tpu as pltpu
from jax.sharding import Mesh, PartitionSpec as P

WIDTH = 128
BLOCK = 64
KW = 4
F32 = jnp.float32
BF16 = jnp.bfloat16
HEADS_PER_STEP = 4
HEADS_PER_END = 4


def dot(a, b, ca, cb):
    return lax.dot_general(a, b, (((ca,), (cb,)), ((), ())), preferred_element_type=F32)


def split(x):
    high = x.astype(BF16)
    return high, (x - high.astype(F32)).astype(BF16)


def cat(parts, axis):
    return jnp.concatenate(parts, axis=axis)


def mm_wide(a, b, cb):
    ah, al = a
    bh, bl = b
    return dot(cat([ah, al], 1), cat([bh, bh], cb), 1, cb) + dot(ah, bl, 1, cb)


def left(a):
    return cat([a[0], a[0], a[1]], 1)


def right(b):
    return cat([b[0], b[1], b[0]], 0)


def front_kernel(heads, q_ref, k_ref, v_ref, rim_ref, beta_ref, cq_ref, ck_ref, cv_ref, tb_ref, qe_ref, ol_ref, pad_ref):
    length = q_ref.shape[0]
    blocks = length // BLOCK
    edge = KW - 1

    def feature(slot, x_ref, w_ref):
        pad = pad_ref.at[slot]
        pad[8 - edge : 8, :] = rim_ref[slot * edge : (slot + 1) * edge, :].astype(F32)
        pad[8:, :] = x_ref[...].astype(F32)
        total = w_ref[0:1, :] * pad[8 - edge : 8 - edge + length, :]
        for j in range(1, KW):
            total = total + w_ref[j : j + 1, :] * pad[8 - edge + j : 8 - edge + j + length, :]
        return total / (1.0 + jnp.exp(-total))

    def unit(x):
        return x * lax.rsqrt(jnp.sum(x * x, axis=-1, keepdims=True) + 1e-06)

    q_all = feature(0, q_ref, cq_ref)
    k_all = feature(1, k_ref, ck_ref)
    v_all = feature(2, v_ref, cv_ref)
    beta = beta_ref[...].astype(F32)
    lane = lax.broadcasted_iota(jnp.int32, beta.shape, 1)
    row = lax.broadcasted_iota(jnp.int32, (BLOCK, BLOCK), 0)
    col = lax.broadcasted_iota(jnp.int32, (BLOCK, BLOCK), 1)
    one = jnp.where(row == col, 1.0, 0.0).astype(F32)
    masks = [
        ((row >> (n + 1)) == (col >> (n + 1))) & (((row >> n) & 1) == 1) & (((col >> n) & 1) == 0)
        for n in range(6)
    ]
    wide_row = lax.broadcasted_iota(jnp.int32, (WIDTH, 2 * WIDTH), 0)
    wide_col = lax.broadcasted_iota(jnp.int32, (WIDTH, 2 * WIDTH), 1)
    wide_one = jnp.where(wide_row == wide_col, 1.0, 0.0).astype(F32)

    units = [(i, c) for i in range(heads) for c in range(blocks)]
    q, k, kv_scaled, b = {}, {}, {}, {}
    for i in range(heads):
        lanes = slice(i * WIDTH, (i + 1) * WIDTH)
        qh, kh, vh = unit(q_all[:, lanes]), unit(k_all[:, lanes]), v_all[:, lanes]
        bh = jnp.sum(jnp.where(lane == pl.program_id(0) * heads + i, beta, 0.0), axis=1, keepdims=True)
        for c in range(blocks):
            rows = slice(c * BLOCK, (c + 1) * BLOCK)
            q[i, c], k[i, c], b[i, c] = qh[rows], kh[rows], bh[rows]
            kv_scaled[i, c] = cat([kh[rows] * bh[rows], vh[rows] * bh[rows]], 1)
    ks = {u: split(k[u]) for u in units}
    gram, score, inv = {}, {}, {}
    for u in units:
        both = mm_wide(split(cat([k[u], q[u]], 0)), ks[u], 1)
        gram[u] = both[:BLOCK] * b[u]
        score[u] = jnp.where(row >= col, both[BLOCK:], 0.0)
        inv[u] = one - jnp.where(masks[0], gram[u], 0.0)
    for n in range(1, 6):
        parts = {u: split(inv[u]) for u in units}
        moved = {u: dot(left(split(jnp.where(masks[n], gram[u], 0.0))), right(parts[u]), 1, 0) for u in units}
        inv = {u: inv[u] - dot(left(parts[u]), right(split(moved[u])), 1, 0) for u in units}
    step, extra, eff, local = {}, {}, {}, {}
    for u in units:
        solved = dot(left(split(inv[u])), right(split(kv_scaled[u])), 1, 0)
        signed = cat([-solved[:, :WIDTH], solved[:, WIDTH:]], 1)
        rhs = right(split(signed))
        kh, kl = ks[u]
        both = wide_one + dot(cat([kh, kh, kl], 0), rhs, 0, 0)
        step[u], extra[u] = both[:, :WIDTH], both
        seen = dot(left(split(score[u])), rhs, 1, 0)
        eff[u], local[u] = q[u] + seen[:, :WIDTH], seen[:, WIDTH:]
    state = {}
    for c in range(blocks):
        rows = slice(c * BLOCK, (c + 1) * BLOCK)
        for i in range(heads):
            lanes = slice(i * WIDTH, (i + 1) * WIDTH)
            u = (i, c)
            if c == 0:
                state[i] = extra[u]
                qe_ref[rows, lanes] = eff[u]
                ol_ref[rows, lanes] = local[u]
                continue
            out = mm_wide(split(cat([step[u], eff[u]], 0)), split(state[i]), 0)
            state[i] = cat([out[:WIDTH, :WIDTH], out[:WIDTH, WIDTH:] + extra[u][:, WIDTH:]], 1)
            qe_ref[rows, lanes] = out[WIDTH:, :WIDTH]
            ol_ref[rows, lanes] = out[WIDTH:, WIDTH:] + local[u]
    half = WIDTH // 2
    for i in range(heads):
        turned = state[i][:, :WIDTH].T
        added = state[i][:, WIDTH:].T
        for s in range(2):
            tb_ref[2 * i + s, :WIDTH, :] = turned
            tb_ref[2 * i + s, WIDTH:, :] = added[s * half : (s + 1) * half]


def joined(first, second):
    out = mm_wide(split(first), split(second[:WIDTH]), 0)
    return out[:WIDTH], out[WIDTH:] + second[WIDTH:]


def gather_kernel(group, seg_ref, loc_ref, grp_ref):
    groups = seg_ref.shape[0] // group
    for g in range(groups):
        loc_ref[g * group] = seg_ref[g * group]
    for j in range(1, group):
        for g in range(groups):
            at = g * group + j
            top, low = joined(loc_ref[at - 1], seg_ref[at])
            loc_ref[at, :WIDTH, :] = top
            loc_ref[at, WIDTH:, :] = low
    run = loc_ref[group - 1]
    grp_ref[0] = run
    for g in range(1, groups):
        run = cat(joined(run, loc_ref[g * group + group - 1]), 0)
        grp_ref[g] = run


def spread_kernel(group, loc_ref, grp_ref, far_ref, out_ref):
    groups = loc_ref.shape[0] // group
    reach = far_ref.shape[0]

    def through(state, place):
        return mm_wide(split(state), split(place[:WIDTH]), 0) + place[WIDTH:]

    begin = far_ref[reach - 1, WIDTH:, :]
    for d in range(reach - 2, -1, -1):
        begin = through(begin, far_ref[d])
    heads_of = [begin] + [through(begin, grp_ref[g]) for g in range(groups - 1)]
    for g in range(groups):
        out_ref[g * group] = heads_of[g]
    for g in range(groups):
        for j in range(1, group):
            out_ref[g * group + j] = through(heads_of[g], loc_ref[g * group + j - 1])


def end_kernel(heads, qe_ref, ol_ref, st_ref, gain_ref, out_ref):
    for i in range(heads):
        lanes = slice(i * WIDTH, (i + 1) * WIDTH)
        full = ol_ref[:, lanes] + mm_wide(split(qe_ref[:, lanes]), split(st_ref[i]), 1)
        mean = jnp.mean(full * full, axis=-1, keepdims=True)
        out_ref[:, lanes] = (full * lax.rsqrt(mean + 1e-05) * gain_ref[...]).astype(BF16)


def shards(sizes, q_in, k_in, v_in, beta, conv_q, conv_k, conv_v, out_gain):
    nx, nz, nc, ny = sizes
    edge = KW - 1
    length, width = q_in.shape
    head_count = beta.shape[1]
    pieces = 2 * head_count
    every = nx * nz * nc * ny
    rim = cat([q_in[-edge:], k_in[-edge:], v_in[-edge:]], 0)
    rim = lax.ppermute(rim, ("x", "z", "c", "y"), [(i, i + 1) for i in range(every - 1)])

    heads = min(HEADS_PER_STEP, head_count)
    wide = heads * WIDTH
    body = pl.BlockSpec((length, wide), lambda i: (0, i))
    taps = pl.BlockSpec((KW, wide), lambda i: (0, i))
    rows = WIDTH + WIDTH // 2
    vmem = pltpu.CompilerParams(vmem_limit_bytes=56 << 20)
    segment, qe, ol = pl.pallas_call(
        functools.partial(front_kernel, heads),
        grid=(head_count // heads,),
        in_specs=[body, body, body, pl.BlockSpec((3 * edge, wide), lambda i: (0, i)),
                  pl.BlockSpec((length, head_count), lambda i: (0, 0)), taps, taps, taps],
        out_specs=[pl.BlockSpec((2 * heads, rows, WIDTH), lambda i: (i, 0, 0)), body, body],
        out_shape=[jax.ShapeDtypeStruct((pieces, rows, WIDTH), F32),
                   jax.ShapeDtypeStruct((length, width), F32),
                   jax.ShapeDtypeStruct((length, width), F32)],
        scratch_shapes=[pltpu.VMEM((3, 8 + length, wide), F32)],
        compiler_params=vmem,
    )(q_in, k_in, v_in, rim, beta, conv_q, conv_k, conv_v)

    around = ("z", "c", "y")
    segment = lax.all_to_all(segment, around, 0, 0, tiled=True)
    loc, grp = pl.pallas_call(
        functools.partial(gather_kernel, ny),
        out_shape=[jax.ShapeDtypeStruct((pieces, rows, WIDTH), F32),
                   jax.ShapeDtypeStruct((pieces // ny, rows, WIDTH), F32)],
        compiler_params=vmem,
    )(segment)
    total = grp[-1]
    far = jnp.stack([
        lax.ppermute(total, "x", [(i, i + d) for i in range(nx - d)]) for d in range(1, nx)
    ])
    states = pl.pallas_call(
        functools.partial(spread_kernel, ny),
        out_shape=jax.ShapeDtypeStruct((pieces, WIDTH // 2, WIDTH), F32),
        compiler_params=vmem,
    )(loc, grp, far)
    states = lax.all_to_all(states, around, 0, 0, tiled=True).reshape(head_count, WIDTH, WIDTH)

    heads = min(HEADS_PER_END, head_count)
    body = pl.BlockSpec((length, heads * WIDTH), lambda i: (0, i))
    return pl.pallas_call(
        functools.partial(end_kernel, heads),
        grid=(head_count // heads,),
        in_specs=[body, body, pl.BlockSpec((heads, WIDTH, WIDTH), lambda i: (i, 0, 0)),
                  pl.BlockSpec((1, WIDTH), lambda i: (0, 0))],
        out_specs=body,
        out_shape=jax.ShapeDtypeStruct((length, width), BF16),
        compiler_params=vmem,
    )(qe, ol, states, out_gain.reshape(1, WIDTH))


def solution(mesh):
    sizes = (4, 4, 2, 4)
    axes = ("x", "z", "c", "y")
    fine = Mesh(mesh.devices.reshape(sizes), axes)
    rows = P(axes, None)
    return jax.shard_map(
        functools.partial(shards, sizes), mesh=fine,
        in_specs=(rows, rows, rows, rows, P(), P(), P(), P()), out_specs=rows, check_vma=False,
    )
```

```python
import functools

import jax
import jax.numpy as jnp
from jax import lax
from jax.experimental import pallas as pl
from jax.experimental.pallas import tpu as pltpu
from jax.sharding import Mesh, PartitionSpec as P

WIDTH = 128
BLOCK = 64
KW = 4
F32 = jnp.float32
BF16 = jnp.bfloat16


def dot(a, b, ca, cb):
    return lax.dot_general(a, b, (((ca,), (cb,)), ((), ())), preferred_element_type=F32)


def split(x):
    high = x.astype(BF16)
    return high, (x - high.astype(F32)).astype(BF16)


def cat(parts, axis):
    return jnp.concatenate(parts, axis=axis)


def mm_wide(a, b, cb):
    ah, al = a
    bh, bl = b
    return dot(cat([ah, al], 1), cat([bh, bh], cb), 1, cb) + dot(ah, bl, 1, cb)


def mm_thin(a, b):
    return dot(a[0], b[0], 1, 0) + dot(a[0], b[1], 1, 0) + dot(a[1], b[0], 1, 0)


def left(a):
    return cat([a[0], a[0], a[1]], 1)


def right(b):
    return cat([b[0], b[1], b[0]], 0)


def rim_kernel(q_ref, k_ref, v_ref, out_ref):
    edge = KW - 1
    for n, ref in enumerate((q_ref, k_ref, v_ref)):
        out_ref[n * edge : (n + 1) * edge, :] = ref[...].astype(F32)[-edge:].astype(BF16)


def front_kernel(heads, q_ref, k_ref, v_ref, rim_ref, beta_ref, cq_ref, ck_ref, cv_ref, tb_ref, qe_ref, ol_ref, pad_ref):
    length = q_ref.shape[0]
    blocks = length // BLOCK
    edge = KW - 1

    def feature(slot, x_ref, w_ref):
        pad = pad_ref.at[slot]
        pad[8 - edge : 8, :] = rim_ref[slot * edge : (slot + 1) * edge, :].astype(F32)
        pad[8:, :] = x_ref[...].astype(F32)
        total = w_ref[0:1, :] * pad[8 - edge : 8 - edge + length, :]
        for j in range(1, KW):
            total = total + w_ref[j : j + 1, :] * pad[8 - edge + j : 8 - edge + j + length, :]
        return total / (1.0 + jnp.exp(-total))

    def unit(x):
        return x * lax.rsqrt(jnp.sum(x * x, axis=-1, keepdims=True) + 1e-06)

    q_all = feature(0, q_ref, cq_ref)
    k_all = feature(1, k_ref, ck_ref)
    v_all = feature(2, v_ref, cv_ref)
    beta = beta_ref[...].astype(F32)
    lane = lax.broadcasted_iota(jnp.int32, beta.shape, 1)
    row = lax.broadcasted_iota(jnp.int32, (BLOCK, BLOCK), 0)
    col = lax.broadcasted_iota(jnp.int32, (BLOCK, BLOCK), 1)
    one = jnp.where(row == col, 1.0, 0.0).astype(F32)
    masks = [
        ((row >> (n + 1)) == (col >> (n + 1))) & (((row >> n) & 1) == 1) & (((col >> n) & 1) == 0)
        for n in range(6)
    ]
    wide_row = lax.broadcasted_iota(jnp.int32, (WIDTH, 2 * WIDTH), 0)
    wide_col = lax.broadcasted_iota(jnp.int32, (WIDTH, 2 * WIDTH), 1)
    wide_one = jnp.where(wide_row == wide_col, 1.0, 0.0).astype(F32)

    units = [(i, c) for i in range(heads) for c in range(blocks)]
    q, k, kv_scaled, b = {}, {}, {}, {}
    for i in range(heads):
        lanes = slice(i * WIDTH, (i + 1) * WIDTH)
        qh, kh, vh = unit(q_all[:, lanes]), unit(k_all[:, lanes]), v_all[:, lanes]
        bh = jnp.sum(jnp.where(lane == pl.program_id(0) * heads + i, beta, 0.0), axis=1, keepdims=True)
        for c in range(blocks):
            rows = slice(c * BLOCK, (c + 1) * BLOCK)
            q[i, c], k[i, c], b[i, c] = qh[rows], kh[rows], bh[rows]
            kv_scaled[i, c] = cat([kh[rows] * bh[rows], vh[rows] * bh[rows]], 1)
    ks = {u: split(k[u]) for u in units}
    gram, score, inv = {}, {}, {}
    for u in units:
        both = mm_wide(split(cat([k[u], q[u]], 0)), ks[u], 1)
        gram[u] = both[:BLOCK] * b[u]
        score[u] = jnp.where(row >= col, both[BLOCK:], 0.0)
        inv[u] = one - jnp.where(masks[0], gram[u], 0.0)
    for n in range(1, 6):
        parts = {u: split(inv[u]) for u in units}
        moved = {u: mm_thin(split(jnp.where(masks[n], gram[u], 0.0)), parts[u]) for u in units}
        inv = {u: inv[u] - mm_thin(parts[u], split(moved[u])) for u in units}
    step, extra, eff, local = {}, {}, {}, {}
    for u in units:
        solved = mm_thin(split(inv[u]), split(kv_scaled[u]))
        signed = cat([-solved[:, :WIDTH], solved[:, WIDTH:]], 1)
        rhs = right(split(signed))
        kh, kl = ks[u]
        both = wide_one + dot(cat([kh, kh, kl], 0), rhs, 0, 0)
        step[u], extra[u] = both[:, :WIDTH], both
        seen = dot(left(split(score[u])), rhs, 1, 0)
        eff[u], local[u] = q[u] + seen[:, :WIDTH], seen[:, WIDTH:]
    state = {}
    for c in range(blocks):
        rows = slice(c * BLOCK, (c + 1) * BLOCK)
        for i in range(heads):
            lanes = slice(i * WIDTH, (i + 1) * WIDTH)
            u = (i, c)
            if c == 0:
                state[i] = extra[u]
                qe_ref[rows, lanes] = eff[u]
                ol_ref[rows, lanes] = local[u]
                continue
            out = mm_wide(split(cat([step[u], eff[u]], 0)), split(state[i]), 0)
            state[i] = cat([out[:WIDTH, :WIDTH], out[:WIDTH, WIDTH:] + extra[u][:, WIDTH:]], 1)
            qe_ref[rows, lanes] = out[WIDTH:, :WIDTH]
            ol_ref[rows, lanes] = out[WIDTH:, WIDTH:] + local[u]
    half = WIDTH // 2
    for i in range(heads):
        turned = state[i][:, :WIDTH].T
        added = state[i][:, WIDTH:].T
        for s in range(2):
            tb_ref[s * heads + i, :half, :] = turned[s * half : (s + 1) * half]
            tb_ref[s * heads + i, half:, :] = added[s * half : (s + 1) * half]


def joined(first, second):
    out = mm_wide(split(first), split(second[:WIDTH]), 0)
    return out[:WIDTH], out[WIDTH:] + second[WIDTH:]


def gather_kernel(group, core_ref, got_ref, other_ref, loc_ref, grp_ref, tot_ref, seg_ref):
    half = WIDTH // 2
    groups = seg_ref.shape[0] // group
    mine = pl.ds(pl.multiple_of(core_ref[0] * half, half), half)
    theirs = pl.ds(pl.multiple_of((1 - core_ref[0]) * half, half), half)
    seg_ref[:, mine, :] = got_ref[:, :half, :]
    seg_ref[:, theirs, :] = other_ref[...]
    seg_ref[:, WIDTH:, :] = got_ref[:, half:, :]
    for g in range(groups):
        loc_ref[g * group] = seg_ref[g * group]
    for j in range(1, group):
        for g in range(groups):
            at = g * group + j
            top, low = joined(loc_ref[at - 1], seg_ref[at])
            loc_ref[at, :WIDTH, :] = top
            loc_ref[at, WIDTH:, :] = low
    run = loc_ref[group - 1]
    grp_ref[0] = run
    for g in range(1, groups):
        run = cat(joined(run, loc_ref[g * group + group - 1]), 0)
        grp_ref[g] = run
    tot_ref[...] = run


def spread_kernel(group, loc_ref, grp_ref, *rest):
    far, out_ref = rest[:-1], rest[-1]
    groups = loc_ref.shape[0] // group

    def through(state, place):
        return mm_wide(split(state), split(place[:WIDTH]), 0) + place[WIDTH:]

    begin = far[-1][WIDTH:, :]
    for place in far[-2::-1]:
        begin = through(begin, place[...])
    heads_of = [begin] + [through(begin, grp_ref[g]) for g in range(groups - 1)]
    for g in range(groups):
        out_ref[g * group] = heads_of[g]
    for g in range(groups):
        for j in range(1, group):
            out_ref[g * group + j] = through(heads_of[g], loc_ref[g * group + j - 1])


def end_kernel(heads, qe_ref, ol_ref, st_ref, gain_ref, out_ref):
    for i in range(heads):
        lanes = slice(i * WIDTH, (i + 1) * WIDTH)
        full = ol_ref[:, lanes] + mm_wide(split(qe_ref[:, lanes]), split(cat([st_ref[i], st_ref[heads + i]], 0)), 1)
        mean = jnp.mean(full * full, axis=-1, keepdims=True)
        out_ref[:, lanes] = (full * lax.rsqrt(mean + 1e-05) * gain_ref[...]).astype(BF16)


def shards(sizes, q_in, k_in, v_in, beta, conv_q, conv_k, conv_v, out_gain):
    nx, nz, nc, ny = sizes
    edge = KW - 1
    length, width = q_in.shape
    head_count = beta.shape[1]
    pieces = 2 * head_count
    every = nx * nz * nc * ny
    last = pl.BlockSpec((16, width), lambda i: (length // 16 - 1, 0))
    rim = pl.pallas_call(
        rim_kernel,
        grid=(1,),
        in_specs=[last] * 3,
        out_specs=pl.BlockSpec((3 * edge, width), lambda i: (0, 0)),
        out_shape=jax.ShapeDtypeStruct((3 * edge, width), BF16),
    )(q_in, k_in, v_in)
    rim = lax.ppermute(rim, ("x", "z", "c", "y"), [(i, i + 1) for i in range(every - 1)])

    heads = head_count // nz
    wide = heads * WIDTH
    body = pl.BlockSpec((length, wide), lambda i: (0, i))
    taps = pl.BlockSpec((KW, wide), lambda i: (0, i))
    rows = WIDTH + WIDTH // 2
    vmem = pltpu.CompilerParams(vmem_limit_bytes=56 << 20)
    segment, qe, ol = pl.pallas_call(
        functools.partial(front_kernel, heads),
        grid=(head_count // heads,),
        in_specs=[body, body, body, pl.BlockSpec((3 * edge, wide), lambda i: (0, i)),
                  pl.BlockSpec((length, head_count), lambda i: (0, 0)), taps, taps, taps],
        out_specs=[pl.BlockSpec((2 * heads, WIDTH, WIDTH), lambda i: (i, 0, 0)), body, body],
        out_shape=[jax.ShapeDtypeStruct((pieces, WIDTH, WIDTH), F32),
                   jax.ShapeDtypeStruct((length, width), F32),
                   jax.ShapeDtypeStruct((length, width), F32)],
        scratch_shapes=[pltpu.VMEM((3, 8 + length, wide), F32)],
        compiler_params=vmem,
    )(q_in, k_in, v_in, rim, beta, conv_q, conv_k, conv_v)

    around = ("z", "c", "y")
    segment = lax.all_to_all(segment, around, 0, 0, tiled=True)
    other = lax.ppermute(segment[:, : WIDTH // 2], "c", [(0, 1), (1, 0)])
    loc, grp, total = pl.pallas_call(
        functools.partial(gather_kernel, ny),
        in_specs=[pl.BlockSpec(memory_space=pltpu.SMEM), pl.BlockSpec(memory_space=pltpu.VMEM),
                  pl.BlockSpec(memory_space=pltpu.VMEM)],
        scratch_shapes=[pltpu.VMEM((pieces, rows, WIDTH), F32)],
        out_shape=[jax.ShapeDtypeStruct((pieces, rows, WIDTH), F32),
                   jax.ShapeDtypeStruct((pieces // ny, rows, WIDTH), F32),
                   jax.ShapeDtypeStruct((rows, WIDTH), F32)],
        compiler_params=vmem,
    )(lax.axis_index("c").astype(jnp.int32).reshape(1), segment, other)
    far = [lax.ppermute(total, "x", [(i, i + d) for i in range(nx - d)]) for d in range(1, nx)]
    states = pl.pallas_call(
        functools.partial(spread_kernel, ny),
        out_shape=jax.ShapeDtypeStruct((pieces, WIDTH // 2, WIDTH), F32),
        compiler_params=vmem,
    )(loc, grp, *far)
    states = lax.all_to_all(states, around, 0, 0, tiled=True)

    heads = head_count // nz
    body = pl.BlockSpec((length, heads * WIDTH), lambda i: (0, i))
    return pl.pallas_call(
        functools.partial(end_kernel, heads),
        grid=(head_count // heads,),
        in_specs=[body, body, pl.BlockSpec((2 * heads, WIDTH // 2, WIDTH), lambda i: (i, 0, 0)),
                  pl.BlockSpec((1, WIDTH), lambda i: (0, 0))],
        out_specs=body,
        out_shape=jax.ShapeDtypeStruct((length, width), BF16),
        compiler_params=vmem,
    )(qe, ol, states, out_gain.reshape(1, WIDTH))


def solution(mesh):
    sizes = (4, 4, 2, 4)
    axes = ("x", "z", "c", "y")
    fine = Mesh(mesh.devices.reshape(sizes), axes)
    rows = P(axes, None)
    return jax.shard_map(
        functools.partial(shards, sizes), mesh=fine,
        in_specs=(rows, rows, rows, rows, P(), P(), P(), P()), out_specs=rows, check_vma=False,
    )
```

```python
import functools

import jax
import jax.numpy as jnp
from jax import lax
from jax.experimental import pallas as pl
from jax.experimental.pallas import tpu as pltpu
from jax.sharding import Mesh, PartitionSpec as P

WIDTH = 128
BLOCK = 64
KW = 4
F32 = jnp.float32
BF16 = jnp.bfloat16


def dot(a, b, ca, cb):
    return lax.dot_general(a, b, (((ca,), (cb,)), ((), ())), preferred_element_type=F32)


def split(x):
    high = x.astype(BF16)
    return high, (x - high.astype(F32)).astype(BF16)


def cat(parts, axis):
    return jnp.concatenate(parts, axis=axis)


def mm_wide(a, b, cb):
    ah, al = a
    bh, bl = b
    return dot(cat([ah, al], 1), cat([bh, bh], cb), 1, cb) + dot(ah, bl, 1, cb)


def mm_thin(a, b):
    return dot(a[0], b[0], 1, 0) + dot(a[0], b[1], 1, 0) + dot(a[1], b[0], 1, 0)


def left(a):
    return cat([a[0], a[0], a[1]], 1)


def right(b):
    return cat([b[0], b[1], b[0]], 0)


def rim_kernel(q_ref, k_ref, v_ref, out_ref):
    edge = KW - 1
    for n, ref in enumerate((q_ref, k_ref, v_ref)):
        out_ref[n * edge : (n + 1) * edge, :] = ref[...].astype(F32)[-edge:].astype(BF16)


def front_kernel(heads, q_ref, k_ref, v_ref, rim_ref, beta_ref, cq_ref, ck_ref, cv_ref, tb_ref, qe_ref, ol_ref, pad_ref):
    length = q_ref.shape[0]
    blocks = length // BLOCK
    edge = KW - 1

    def feature(slot, x_ref, w_ref):
        pad = pad_ref.at[slot]
        pad[8 - edge : 8, :] = rim_ref[slot * edge : (slot + 1) * edge, :].astype(F32)
        pad[8:, :] = x_ref[...].astype(F32)
        total = w_ref[0:1, :] * pad[8 - edge : 8 - edge + length, :]
        for j in range(1, KW):
            total = total + w_ref[j : j + 1, :] * pad[8 - edge + j : 8 - edge + j + length, :]
        return total / (1.0 + jnp.exp(-total))

    def unit(x):
        return x * lax.rsqrt(jnp.sum(x * x, axis=-1, keepdims=True) + 1e-06)

    q_all = feature(0, q_ref, cq_ref)
    k_all = feature(1, k_ref, ck_ref)
    v_all = feature(2, v_ref, cv_ref)
    beta = beta_ref[...].astype(F32)
    lane = lax.broadcasted_iota(jnp.int32, beta.shape, 1)
    row = lax.broadcasted_iota(jnp.int32, (BLOCK, BLOCK), 0)
    col = lax.broadcasted_iota(jnp.int32, (BLOCK, BLOCK), 1)
    one = jnp.where(row == col, 1.0, 0.0).astype(F32)
    masks = [
        ((row >> (n + 1)) == (col >> (n + 1))) & (((row >> n) & 1) == 1) & (((col >> n) & 1) == 0)
        for n in range(6)
    ]
    wide_row = lax.broadcasted_iota(jnp.int32, (WIDTH, 2 * WIDTH), 0)
    wide_col = lax.broadcasted_iota(jnp.int32, (WIDTH, 2 * WIDTH), 1)
    wide_one = jnp.where(wide_row == wide_col, 1.0, 0.0).astype(F32)

    units = [(i, c) for i in range(heads) for c in range(blocks)]
    q, k, kv_scaled, b = {}, {}, {}, {}
    for i in range(heads):
        lanes = slice(i * WIDTH, (i + 1) * WIDTH)
        qh, kh, vh = unit(q_all[:, lanes]), unit(k_all[:, lanes]), v_all[:, lanes]
        bh = jnp.sum(jnp.where(lane == pl.program_id(0) * heads + i, beta, 0.0), axis=1, keepdims=True)
        for c in range(blocks):
            rows = slice(c * BLOCK, (c + 1) * BLOCK)
            q[i, c], k[i, c], b[i, c] = qh[rows], kh[rows], bh[rows]
            kv_scaled[i, c] = cat([kh[rows] * bh[rows], vh[rows] * bh[rows]], 1)
    ks = {u: split(k[u]) for u in units}
    gram, score, inv = {}, {}, {}
    for u in units:
        both = mm_wide(split(cat([k[u], q[u]], 0)), ks[u], 1)
        gram[u] = both[:BLOCK] * b[u]
        score[u] = jnp.where(row >= col, both[BLOCK:], 0.0)
        inv[u] = one - jnp.where(masks[0], gram[u], 0.0)
    for n in range(1, 6):
        parts = {u: split(inv[u]) for u in units}
        moved = {u: mm_thin(split(jnp.where(masks[n], gram[u], 0.0)), parts[u]) for u in units}
        inv = {u: inv[u] - mm_thin(parts[u], split(moved[u])) for u in units}
    step, extra, eff, local = {}, {}, {}, {}
    for u in units:
        solved = mm_thin(split(inv[u]), split(kv_scaled[u]))
        signed = cat([-solved[:, :WIDTH], solved[:, WIDTH:]], 1)
        rhs = right(split(signed))
        kh, kl = ks[u]
        both = wide_one + dot(cat([kh, kh, kl], 0), rhs, 0, 0)
        step[u], extra[u] = both[:, :WIDTH], both
        seen = dot(left(split(score[u])), rhs, 1, 0)
        eff[u], local[u] = q[u] + seen[:, :WIDTH], seen[:, WIDTH:]
    state = {}
    for c in range(blocks):
        rows = slice(c * BLOCK, (c + 1) * BLOCK)
        for i in range(heads):
            lanes = slice(i * WIDTH, (i + 1) * WIDTH)
            u = (i, c)
            if c == 0:
                state[i] = extra[u]
                qe_ref[rows, lanes] = eff[u]
                ol_ref[rows, lanes] = local[u]
                continue
            out = mm_wide(split(cat([step[u], eff[u]], 0)), split(state[i]), 0)
            state[i] = cat([out[:WIDTH, :WIDTH], out[:WIDTH, WIDTH:] + extra[u][:, WIDTH:]], 1)
            qe_ref[rows, lanes] = out[WIDTH:, :WIDTH]
            ol_ref[rows, lanes] = out[WIDTH:, WIDTH:] + local[u]
    half = WIDTH // 2
    for i in range(heads):
        turned = state[i][:, :WIDTH].T
        added = state[i][:, WIDTH:].T
        for s in range(2):
            tb_ref[s * heads + i, :half, :] = turned[s * half : (s + 1) * half]
            tb_ref[s * heads + i, half:, :] = added[s * half : (s + 1) * half]


def joined(first, second):
    out = mm_wide(split(first), split(second[:WIDTH]), 0)
    return out[:WIDTH], out[WIDTH:] + second[WIDTH:]


def gather_kernel(group, core_ref, got_ref, other_ref, loc_ref, grp_ref, tot_ref, seg_ref):
    half = WIDTH // 2
    groups = seg_ref.shape[0] // group
    mine = pl.ds(pl.multiple_of(core_ref[0] * half, half), half)
    theirs = pl.ds(pl.multiple_of((1 - core_ref[0]) * half, half), half)
    seg_ref[:, mine, :] = got_ref[:, :half, :]
    seg_ref[:, theirs, :] = other_ref[...]
    seg_ref[:, WIDTH:, :] = got_ref[:, half:, :]
    for g in range(groups):
        loc_ref[g * group] = seg_ref[g * group]
    for j in range(1, group):
        for g in range(groups):
            at = g * group + j
            top, low = joined(loc_ref[at - 1], seg_ref[at])
            loc_ref[at, :WIDTH, :] = top
            loc_ref[at, WIDTH:, :] = low
    run = loc_ref[group - 1]
    grp_ref[0] = run
    for g in range(1, groups):
        run = cat(joined(run, loc_ref[g * group + group - 1]), 0)
        grp_ref[g] = run
    tot_ref[...] = run


def spread_kernel(group, loc_ref, grp_ref, *rest):
    far, out_ref = rest[:-1], rest[-1]
    groups = loc_ref.shape[0] // group

    def through(state, place):
        return mm_wide(split(state), split(place[:WIDTH]), 0) + place[WIDTH:]

    begin = far[-1][WIDTH:, :]
    for place in far[-2::-1]:
        begin = through(begin, place[...])
    heads_of = [begin] + [through(begin, grp_ref[g]) for g in range(groups - 1)]
    for g in range(groups):
        out_ref[g * group] = heads_of[g]
    for g in range(groups):
        for j in range(1, group):
            out_ref[g * group + j] = through(heads_of[g], loc_ref[g * group + j - 1])


def end_kernel(heads, qe_ref, ol_ref, st_ref, gain_ref, out_ref):
    for i in range(heads):
        lanes = slice(i * WIDTH, (i + 1) * WIDTH)
        full = ol_ref[:, lanes] + mm_wide(split(qe_ref[:, lanes]), split(cat([st_ref[i], st_ref[heads + i]], 0)), 1)
        mean = jnp.mean(full * full, axis=-1, keepdims=True)
        out_ref[:, lanes] = (full * lax.rsqrt(mean + 1e-05) * gain_ref[...]).astype(BF16)


def shards(sizes, q_in, k_in, v_in, beta, conv_q, conv_k, conv_v, out_gain):
    nx, nz, nc, ny = sizes
    edge = KW - 1
    length, width = q_in.shape
    head_count = beta.shape[1]
    pieces = 2 * head_count
    every = nx * nz * nc * ny
    last = pl.BlockSpec((16, width), lambda i: (length // 16 - 1, 0))
    rim = pl.pallas_call(
        rim_kernel,
        grid=(1,),
        in_specs=[last] * 3,
        out_specs=pl.BlockSpec((3 * edge, width), lambda i: (0, 0)),
        out_shape=jax.ShapeDtypeStruct((3 * edge, width), BF16),
    )(q_in, k_in, v_in)
    rim = lax.ppermute(rim, ("x", "z", "c", "y"), [(i, i + 1) for i in range(every - 1)])

    heads = head_count // nz
    wide = heads * WIDTH
    body = pl.BlockSpec((length, wide), lambda i: (0, i))
    taps = pl.BlockSpec((KW, wide), lambda i: (0, i))
    rows = WIDTH + WIDTH // 2
    vmem = pltpu.CompilerParams(vmem_limit_bytes=56 << 20)
    small = pltpu.CompilerParams(vmem_limit_bytes=20 << 20)
    segment, qe, ol = pl.pallas_call(
        functools.partial(front_kernel, heads),
        grid=(head_count // heads,),
        in_specs=[body, body, body, pl.BlockSpec((3 * edge, wide), lambda i: (0, i)),
                  pl.BlockSpec((length, head_count), lambda i: (0, 0)), taps, taps, taps],
        out_specs=[pl.BlockSpec((2 * heads, WIDTH, WIDTH), lambda i: (i, 0, 0)), body, body],
        out_shape=[jax.ShapeDtypeStruct((pieces, WIDTH, WIDTH), F32),
                   jax.ShapeDtypeStruct((length, width), F32),
                   jax.ShapeDtypeStruct((length, width), F32)],
        scratch_shapes=[pltpu.VMEM((3, 8 + length, wide), F32)],
        compiler_params=vmem,
    )(q_in, k_in, v_in, rim, beta, conv_q, conv_k, conv_v)

    around = ("z", "c", "y")
    segment = lax.all_to_all(segment, around, 0, 0, tiled=True)
    other = lax.ppermute(segment[:, : WIDTH // 2], "c", [(0, 1), (1, 0)])
    loc, grp, total = pl.pallas_call(
        functools.partial(gather_kernel, ny),
        in_specs=[pl.BlockSpec(memory_space=pltpu.SMEM), pl.BlockSpec(memory_space=pltpu.VMEM),
                  pl.BlockSpec(memory_space=pltpu.VMEM)],
        scratch_shapes=[pltpu.VMEM((pieces, rows, WIDTH), F32)],
        out_shape=[jax.ShapeDtypeStruct((pieces, rows, WIDTH), F32),
                   jax.ShapeDtypeStruct((pieces // ny, rows, WIDTH), F32),
                   jax.ShapeDtypeStruct((rows, WIDTH), F32)],
        compiler_params=small,
    )(lax.axis_index("c").astype(jnp.int32).reshape(1), segment, other)
    far = [lax.ppermute(total, "x", [(i, i + d) for i in range(nx - d)]) for d in range(1, nx)]
    states = pl.pallas_call(
        functools.partial(spread_kernel, ny),
        out_shape=jax.ShapeDtypeStruct((pieces, WIDTH // 2, WIDTH), F32),
        compiler_params=small,
    )(loc, grp, *far)
    states = lax.all_to_all(states, around, 0, 0, tiled=True)

    heads = head_count // nz
    body = pl.BlockSpec((length, heads * WIDTH), lambda i: (0, i))
    return pl.pallas_call(
        functools.partial(end_kernel, heads),
        grid=(head_count // heads,),
        in_specs=[body, body, pl.BlockSpec((2 * heads, WIDTH // 2, WIDTH), lambda i: (i, 0, 0)),
                  pl.BlockSpec((1, WIDTH), lambda i: (0, 0))],
        out_specs=body,
        out_shape=jax.ShapeDtypeStruct((length, width), BF16),
        compiler_params=small,
    )(qe, ol, states, out_gain.reshape(1, WIDTH))


def solution(mesh):
    sizes = (4, 4, 2, 4)
    axes = ("x", "z", "c", "y")
    fine = Mesh(mesh.devices.reshape(sizes), axes)
    rows = P(axes, None)
    return jax.shard_map(
        functools.partial(shards, sizes), mesh=fine,
        in_specs=(rows, rows, rows, rows, P(), P(), P(), P()), out_specs=rows, check_vma=False,
    )
```
